256 devices in a mesh: grp: 8 (over z_lo, x), dev: 32 (over z_hi, y, core).
Axes of the slice: x: 4, y: 4, z: 8 (z_hi: 4, z_lo: 2; z = z_hi * 2 + z_lo), core: 2. Of those that a mesh axis runs over, the one named last changes fastest.
Arguments:
- pair_ft: bfloat16 [8192, 2, 4096], P('dev', None, 'grp'), may hold values from -6 to 6
- aux_ft: bfloat16 [4096, 2, 4096], P('dev', None, 'grp'), may hold values from -0.0625 to 0.0625
- coul_weight: float32 [4096], P('grp'), may hold values from 0.2 to 5
- aux_basis: bfloat16 [128, 4096], replicated, may hold values from -0.5 to 0.5
- aux_decay: float32 [4096], replicated, may hold values from 0.05 to 1
- image_dist: float32 [125], replicated, may hold values from 0 to 3
- image_phase: float32 [125], replicated, may hold values from -3.140625 to 3.140625
- item_pair: bfloat16 [4096, 128, 128], P(('grp', 'dev')), may hold values from -4 to 4
- item_image: int32 [4096], P(('grp', 'dev')), may hold values from 0 to 124
- item_sub: int32 [4096], P(('grp', 'dev')), may hold values from 0 to 1
- item_count: int32 [256], P(('grp', 'dev')), may hold values from 0 to 16, as said below
Outputs:
- j3c: bfloat16 [4096, 2, 8192], P('grp', None, 'dev')
The draws below stay inside these ranges and needn't reach their ends.
Inputs may be any that keep to these rules, and one draw needn't show every extreme that they name: `item_count`: in every index of dev one of the 8 devices holds exactly 16 live slots. The counts of the 8 devices that share an index of dev sum to at most 72, and in every draw some index of dev reaches 72.
All inputs are finite; a program needn't handle non-finite values.
Results may differ from the reference program's by a relative error of at most 0.0047.
Values may be sent and summed in bfloat16 or wider, within the bound.
A program may use at most 64 MiB of HBM per device.

```python
import math
import jax
import jax.numpy as jnp
from jax import lax

NAUX = 4096
KRANK = 128
SUB_ROWS = 128
NIMG = 125
CAP = 16
ROW_DEV = 256
GROUPS = 8
BLOCKS = 32
NPAIR = 8192
NG = 4096
SUBS = 2
DEVICES = 256


def draw_item_count(key, part):
    subkeys = jax.random.split(jax.random.fold_in(key, 17), 3)
    others = jax.random.randint(subkeys[0], (GROUPS, BLOCKS), 0, 9)
    busiest = jax.random.randint(subkeys[1], (BLOCKS,), 0, GROUPS)
    fullest = jax.random.randint(subkeys[2], (), 0, BLOCKS)
    group_ids = jnp.arange(GROUPS, dtype=jnp.int32)[:, None]
    column_ids = jnp.arange(BLOCKS, dtype=jnp.int32)[None, :]
    others = jnp.where(column_ids == fullest, 8, others)
    counts = jnp.where(group_ids == busiest[None, :], CAP, others)
    return counts.reshape(GROUPS * BLOCKS).astype(jnp.int32)


def with_ends(drawn, stream_key, low, largest):
    place = [jax.random.randint(jax.random.fold_in(stream_key, axis), (), 0, length) for axis, length in enumerate(drawn.shape)]
    widest = drawn.shape.index(max(drawn.shape))
    next_to = place[:widest] + [(place[widest] + 1) % drawn.shape[widest]] + place[widest + 1:]
    return drawn.at[tuple(place)].set(low).at[tuple(next_to)].set(largest)


def level_of(stream_key, extent, cuts, least, largest):
    loudness = 1.0
    for dim, parts in cuts:
        steps = jax.random.uniform(jax.random.fold_in(jax.random.fold_in(stream_key, 6), dim), (parts,), jnp.float32, least / len(cuts), largest / len(cuts))
        loudness = loudness * jnp.repeat(jnp.exp(steps), extent[dim] // parts).reshape((-1,) + (1,) * (len(extent) - 1 - dim))
    return loudness


def scatter_about(rng, dims, scale, reach, shards=(), held_as=jnp.bfloat16):
    loudness = level_of(rng, dims, shards, -0.22, 0.18) if shards else 1.0
    entries = jax.random.normal(rng, dims, jnp.float32) * scale * loudness
    return jnp.minimum(jnp.maximum(entries, -reach), reach).astype(held_as)


def setup_inputs(seed: int = 0) -> dict:
    streams_of = jax.random.split(jax.random.key(seed), 12)
    pair_ft = scatter_about(streams_of[0], (NPAIR, 2, NG), 1.0, 6.0, ((0, 32), (2, 8)))
    aux_ft = scatter_about(streams_of[1], (NAUX, 2, NG), (2 * NG) ** -0.5, 0.0625, ((0, 32), (2, 8)))
    coul_weight = jnp.clip(jnp.exp(math.log(5.0) - 3.218876 * jax.random.uniform(streams_of[2], (NG,), jnp.float32) ** level_of(streams_of[2], (NG,), ((0, 8),), -0.2, 0.2)), 0.2, 5.0)
    aux_basis = scatter_about(streams_of[3], (KRANK, NAUX), KRANK ** -0.5, 0.5)
    aux_decay = jnp.clip(jnp.exp(jax.random.uniform(streams_of[4], (NAUX,), jnp.float32, math.log(0.05), math.log(1.0))), 0.05, 1.0)
    image_dist = jnp.clip(jax.random.uniform(streams_of[5], (NIMG,), jnp.float32, 0.0, 3.0), 0.0, 3.0)
    image_phase = jnp.clip(jax.random.uniform(streams_of[6], (NIMG,), jnp.float32, -3.140625, 3.140625), -3.140625, 3.140625)
    item_pair = scatter_about(streams_of[7], (DEVICES * CAP, KRANK, SUB_ROWS), 0.3, 4.0, ((0, 256),))
    item_image = with_ends(jax.random.randint(streams_of[8], (DEVICES * CAP,), 0, NIMG), jax.random.fold_in(streams_of[8], 1), 0, NIMG - 1).astype(jnp.int32)
    item_sub = with_ends(jax.random.randint(streams_of[9], (DEVICES * CAP,), 0, SUBS), jax.random.fold_in(streams_of[9], 1), 0, SUBS - 1).astype(jnp.int32)
    item_count = draw_item_count(jax.random.fold_in(streams_of[11], 71), 0)
    return {"pair_ft": pair_ft, "aux_ft": aux_ft, "coul_weight": coul_weight, "aux_basis": aux_basis, "aux_decay": aux_decay, "image_dist": image_dist, "image_phase": image_phase, "item_pair": item_pair, "item_image": item_image, "item_sub": item_sub, "item_count": item_count}


def reference(pair_ft, aux_ft, coul_weight, aux_basis, aux_decay, image_dist, image_phase, item_pair, item_image, item_sub, item_count):
    weighted = (pair_ft.astype(jnp.float32) * coul_weight[None, None, :]).astype(jnp.bfloat16)
    weighted = lax.optimization_barrier(weighted).astype(jnp.float32)
    real_part = weighted[:, 0, :].T
    imag_part = weighted[:, 1, :].T
    real_cols = jnp.concatenate([real_part, imag_part], axis=0)
    imag_cols = jnp.concatenate([imag_part, -real_part], axis=0)
    pair_matrix = jnp.concatenate([real_cols, imag_cols], axis=1)
    aux_rows = aux_ft.astype(jnp.float32).reshape(NAUX, 2 * NG)
    long_range = jnp.dot(aux_rows, pair_matrix, precision=lax.Precision.HIGHEST).reshape(NAUX, 2, NPAIR)
    basis_full = aux_basis.astype(jnp.float32)

    def add_item(running, slot_index):
        device = slot_index // CAP
        slot_pos = slot_index % CAP
        column = device % BLOCKS
        usable = slot_pos < item_count[device]

        def compute(current_sum):
            pair_block = item_pair[slot_index].astype(jnp.float32)
            product = jnp.dot(basis_full.T, pair_block, precision=lax.Precision.HIGHEST)
            image_now = item_image[slot_index]
            damping = jnp.exp(-aux_decay * image_dist[image_now])
            phase_value = image_phase[image_now]
            contribution = jnp.stack([jnp.cos(phase_value) * damping[:, None] * product, jnp.sin(phase_value) * damping[:, None] * product], axis=1)
            first_row = (column * ROW_DEV + item_sub[slot_index] * SUB_ROWS).astype(jnp.int32)
            anchor = (jnp.int32(0), jnp.int32(0), first_row)
            current = lax.dynamic_slice(current_sum, anchor, (NAUX, 2, SUB_ROWS))
            return lax.dynamic_update_slice(current_sum, current + contribution, anchor)

        def unchanged(current_sum):
            return current_sum

        return lax.cond(usable, compute, unchanged, running), None

    short_range, _ = lax.scan(add_item, jnp.zeros((NAUX, 2, NPAIR), jnp.float32), jnp.arange(DEVICES * CAP, dtype=jnp.int32))
    return (long_range + short_range).astype(jnp.bfloat16)
```

```python
import jax
import jax.numpy as jnp
from jax import lax
from jax.experimental import pallas as pl
from jax.experimental.pallas import tpu as pltpu
from jax.sharding import PartitionSpec as P

MESH = pl.DeviceIdType.MESH
HALVES = 2
SIDE = 4
ORDER = ((0, 0), (0, 1), (1, 0), (2, 0), (1, 1), (2, 1), (3, 0), (3, 1))
STEP_OF = {entry: index for index, entry in enumerate(ORDER)}
STEPS = len(ORDER)


def offset_of(index):
    high = index // 2
    return 2 * high + (high + index) % 2


def wrap(value):
    return lax.rem(value + 8, 4)


def kernel(
    aux_ref,
    pair_ref,
    basis_ref,
    decay_ref,
    items_ref,
    dist_ref,
    phase_ref,
    image_ref,
    sub_ref,
    count_ref,
    out_ref,
    factors,
    total,
    ring_in,
    ring_out,
    pair_in,
    long_rhs,
    short_rhs,
    basis_rows,
    decay_rows,
    damped,
    scales,
    load_sem,
    factor_recv,
    z_send,
    z_relay,
    y_send,
    y_relay,
    core_send,
    ring_send,
    ring_recv,
    pair_recv,
):
    group, member = lax.axis_index("grp"), lax.axis_index("dev")
    z_low, x = lax.div(group, 4), lax.rem(group, 4)
    core, y, z = lax.rem(member, 2), lax.rem(lax.div(member, 2), 4), lax.div(member, 8)
    way = 1 - 2 * core
    piece = factors.shape[3]
    items = items_ref.shape[0]
    rank = items_ref.shape[1]
    columns = long_rhs.shape[0]
    side_rows = columns // 2
    half_k = pair_ref.shape[1] // 2

    def place(z_at, y_at, core_at):
        return (group, (z_at * 4 + y_at) * 2 + core_at)

    own = z * 4 + y
    for half in range(HALVES):
        pltpu.make_async_copy(
            aux_ref.at[pl.ds(half * piece, piece)], factors.at[half, own, core], load_sem.at[half]
        ).start()

    peers = (
        place(wrap(z + 1), y, core),
        place(wrap(z - 1), y, core),
        place(z, wrap(y + 1), core),
        place(z, wrap(y - 1), core),
        place(z, y, 1 - core),
        (z_low * 4 + wrap(x + 1), member),
        (z_low * 4 + wrap(x - 1), member),
        ((1 - z_low) * 4 + x, member),
    )
    barrier = pltpu.get_barrier_semaphore()
    for peer in peers:
        pl.semaphore_signal(barrier, inc=1, device_id=peer, device_id_type=MESH)
    pl.semaphore_wait(barrier, len(peers))

    def factor_copy(half, chip, core_at, target, send_sem):
        return pltpu.make_async_remote_copy(
            src_ref=factors.at[half, chip, core_at],
            dst_ref=factors.at[half, chip, core_at],
            send_sem=send_sem,
            recv_sem=factor_recv.at[half * 32 + chip * 2 + core_at],
            device_id=target,
            device_id_type=MESH,
        )

    def await_factor(half, chip, core_at):
        factor_copy(half, chip, core_at, peers[4], load_sem.at[0]).wait_recv()

    waits = []

    def send(half, chip, target, send_sem):
        copy = factor_copy(half, chip, core, target, send_sem)
        copy.start()
        waits.append(copy)

    def chip_at(z_step, y_step):
        return wrap(z + offset_of(z_step)) * 4 + wrap(y + y_step)

    def relay_column(step):
        z_step, half = ORDER[step]
        chip = chip_at(z_step, 0)
        if z_step == 0:
            pltpu.make_async_copy(
                aux_ref.at[pl.ds(half * piece, piece)], factors.at[half, own, core], load_sem.at[half]
            ).wait()
            send(half, chip, peers[0], z_send.at[half * 2])
            send(half, chip, peers[1], z_send.at[half * 2 + 1])
        else:
            await_factor(half, chip, core)
        send(half, chip, peers[2], y_send.at[step * 2])
        send(half, chip, peers[3], y_send.at[step * 2 + 1])
        if z_step == 1 or z_step == 2:
            onward = peers[1] if z_step == 1 else peers[0]

            @pl.when(core == 2 - z_step)
            def _():
                factor_copy(half, chip, core, onward, z_relay.at[half]).start()

        send(half, chip, peers[4], core_send.at[step * 4])

    def relay_row(step):
        z_step, half = ORDER[step]
        behind, ahead = chip_at(z_step, -way), chip_at(z_step, way)
        await_factor(half, behind, core)
        send(half, behind, place(z, wrap(y + way), core), y_relay.at[step])
        send(half, behind, peers[4], core_send.at[step * 4 + 1])
        await_factor(half, ahead, core)
        send(half, ahead, peers[4], core_send.at[step * 4 + 2])

    def relay_far(step):
        z_step, half = ORDER[step]
        far = chip_at(z_step, 2)
        await_factor(half, far, core)
        send(half, far, peers[4], core_send.at[step * 4 + 3])

    def prepare():
        long_rhs[0:side_rows, :] = pair_ref[...]
        long_rhs[side_rows:columns, 0:half_k] = pair_ref[:, half_k:]
        long_rhs[side_rows:columns, half_k:] = -pair_ref[:, 0:half_k]

        def transpose(index, carry):
            rows = pl.ds(pl.multiple_of(index * 128, 128), 128)
            basis_rows[rows, :] = basis_ref[:, rows].astype(jnp.float32).T
            decay_rows[rows, :] = jnp.broadcast_to(decay_ref[pl.ds(index, 1), :], (128, 128)).T
            return carry

        lax.fori_loop(0, basis_rows.shape[0] // 128, transpose, 0)

        slot = lax.broadcasted_iota(jnp.int32, (items, 128), 0)
        phases = jnp.zeros((items, 128), jnp.float32)
        first = jnp.zeros((items, 128), jnp.float32)
        second = jnp.zeros((items, 128), jnp.float32)
        for index in range(items):
            alive = jnp.where(index < count_ref[0], 1.0, 0.0)
            to_second = sub_ref[index].astype(jnp.float32)
            phases = jnp.where(slot == index, phase_ref[image_ref[index]], phases)
            first = jnp.where(slot == index, alive * (1.0 - to_second), first)
            second = jnp.where(slot == index, alive * to_second, second)
        cosine, sine = jnp.cos(phases), jnp.sin(phases)
        scales[0] = cosine * first
        scales[1] = cosine * second
        scales[2] = sine * first
        scales[3] = sine * second

        def place_item(index, carry):
            block = items_ref[index].astype(jnp.float32)
            rows = pl.ds(pl.multiple_of(index * rank, rank), rank)
            for part in range(4):
                short_rhs[rows, part * 128 : (part + 1) * 128] = (
                    block * scales[part, pl.ds(index, 1), :]
                ).astype(jnp.bfloat16)
            return carry

        lax.fori_loop(0, items, place_item, 0)

    def short_range(z_step):
        def one(y_step, carry):
            chip = chip_at(z_step, offset_of(y_step))
            rows = pl.ds(pl.multiple_of(chip * 4 * piece, 4 * piece), 4 * piece)
            for index in range(items):
                weight = jnp.exp(decay_rows[rows, :] * (-dist_ref[image_ref[index]]))
                damped[:, index * rank : (index + 1) * rank] = (weight * basis_rows[rows, :]).astype(
                    jnp.bfloat16
                )
            product = jnp.dot(damped[...], short_rhs[...], preferred_element_type=jnp.float32)
            for half in range(HALVES):
                for core_at in range(2):
                    start = (core_at * HALVES + half) * piece
                    total[STEP_OF[z_step, half] * 4 + y_step, core_at * piece : (core_at + 1) * piece, :] = (
                        product[start : start + piece]
                    )
            return carry

        lax.fori_loop(0, SIDE, one, 0)

    def long_range(step):
        z_step, half = ORDER[step]

        def one(y_step, carry):
            chip = chip_at(z_step, offset_of(y_step))
            await_factor(half, chip, 1 - core)
            rows = factors[half, chip].reshape(2 * piece, 2 * half_k)
            total[step * 4 + y_step] += lax.dot_general(
                rows, long_rhs[...], (((1,), (1,)), ((), ())), preferred_element_type=jnp.float32
            )
            return carry

        lax.fori_loop(0, SIDE, one, 0)

    def roles(step, y_step):
        z_step, _ = ORDER[step]
        z_at = wrap(z + offset_of(z_step))
        y_at = wrap(y + offset_of(y_step))
        x_at = lax.rem(z_at, 2) * 2 + lax.div(y_at, 2)
        hop = wrap((x - x_at) * way - 1)
        return hop, lax.div(z_at, 2) == z_low, lax.rem(y_at, 2)

    def ring_copy(block):
        return pltpu.make_async_remote_copy(
            src_ref=ring_out.at[block],
            dst_ref=ring_in.at[block],
            send_sem=ring_send.at[block],
            recv_sem=ring_recv.at[block],
            device_id=(z_low * 4 + wrap(x + way), member),
            device_id_type=MESH,
        )

    def pair_copy(block):
        return pltpu.make_async_remote_copy(
            src_ref=ring_out.at[block],
            dst_ref=pair_in.at[block],
            send_sem=ring_send.at[block],
            recv_sem=pair_recv.at[block],
            device_id=peers[7],
            device_id_type=MESH,
        )

    def reduce_hops(step):
        def one(y_step, carry):
            for lag in range(5):
                at = step - lag
                if at < 0 or at >= STEPS:
                    continue
                block = at * 4 + y_step
                hop, keeps, odd_y = roles(at, y_step)
                if lag == 0:

                    @pl.when(hop == 0)
                    def _():
                        ring_out[block] = total[block].astype(jnp.bfloat16)
                        ring_copy(block).start()

                elif lag < 3:

                    @pl.when(hop == lag)
                    def _():
                        ring_copy(block).wait_recv()
                        ring_out[block] = (total[block] + ring_in[block].astype(jnp.float32)).astype(
                            jnp.bfloat16
                        )
                        ring_copy(block).start()

                elif lag == 3:

                    @pl.when((hop == 3) & keeps)
                    def _():
                        ring_copy(block).wait_recv()
                        total[block] += ring_in[block].astype(jnp.float32)

                    @pl.when((hop == 3) & jnp.logical_not(keeps))
                    def _():
                        ring_copy(block).wait_recv()
                        ring_out[block] = (total[block] + ring_in[block].astype(jnp.float32)).astype(
                            jnp.bfloat16
                        )
                        pair_copy(block).start()

                else:
                    _, half = ORDER[at]

                    @pl.when((hop == 3) & keeps)
                    def _():
                        pair_copy(block).wait_recv()
                        done = (total[block] + pair_in[block].astype(jnp.float32)).astype(jnp.bfloat16)
                        for core_at in range(2):
                            start = odd_y * (4 * piece) + (core_at * HALVES + half) * piece
                            out_ref[pl.ds(pl.multiple_of(start, piece), piece), :] = done[
                                core_at * piece : (core_at + 1) * piece
                            ]

            return carry

        lax.fori_loop(0, SIDE, one, 0)

    relay_column(0)
    relay_column(1)
    prepare()
    short_range(0)
    relay_row(0)
    relay_row(1)
    relay_column(2)
    relay_column(3)
    short_range(1)
    for step in range(STEPS + 4):
        if step + 3 < STEPS and step > 0:
            relay_column(step + 3)
        if step + 1 < STEPS and step > 0:
            relay_row(step + 1)
        if step < STEPS:
            relay_far(step)
            long_range(step)
        reduce_hops(step)
        if step < 2:
            short_range(step + 2)

    for copy in waits:
        copy.wait_send()
    for z_step in (1, 2):
        for half in range(HALVES):

            @pl.when(core == 2 - z_step)
            def _():
                factor_copy(half, own, core, peers[0], z_relay.at[half]).wait_send()

    for step in range(STEPS):

        def drain(y_step, carry):
            hop, keeps, _ = roles(step, y_step)

            @pl.when((hop < 3) | jnp.logical_not(keeps))
            def _():
                ring_copy(step * 4 + y_step).wait_send()

            return carry

        lax.fori_loop(0, SIDE, drain, 0)


def body(
    pair_ft,
    aux_ft,
    coul_weight,
    aux_basis,
    aux_decay,
    image_dist,
    image_phase,
    item_pair,
    item_image,
    item_sub,
    item_count,
):
    rows, _, depth = pair_ft.shape
    share = aux_ft.shape[0]
    aux_rows = aux_basis.shape[1]
    capacity, rank, _ = item_pair.shape
    columns = 2 * rows
    piece = share // HALVES
    weighted = (pair_ft.astype(jnp.float32) * coul_weight[None, None, :]).astype(jnp.bfloat16)
    pair_rows = weighted.reshape(rows, 2 * depth)
    factors = aux_ft.reshape(share, 2 * depth)
    blocks = STEPS * SIDE
    vmem = pl.BlockSpec(memory_space=pltpu.VMEM)
    smem = pl.BlockSpec(memory_space=pltpu.SMEM)
    dma = pltpu.SemaphoreType.DMA
    result = pl.pallas_call(
        kernel,
        out_shape=jax.ShapeDtypeStruct((aux_rows // lax.axis_size("grp"), columns), jnp.bfloat16),
        in_specs=[pl.BlockSpec(memory_space=pl.ANY)] + [vmem] * 4 + [smem] * 5,
        out_specs=vmem,
        scratch_shapes=[
            pltpu.VMEM((HALVES, 16, 2, piece, 2 * depth), jnp.bfloat16),
            pltpu.VMEM((blocks, 2 * piece, columns), jnp.float32),
            pltpu.VMEM((blocks, 2 * piece, columns), jnp.bfloat16),
            pltpu.VMEM((blocks, 2 * piece, columns), jnp.bfloat16),
            pltpu.VMEM((blocks, 2 * piece, columns), jnp.bfloat16),
            pltpu.VMEM((columns, 2 * depth), jnp.bfloat16),
            pltpu.VMEM((capacity * rank, columns), jnp.bfloat16),
            pltpu.VMEM((aux_rows, rank), jnp.float32),
            pltpu.VMEM((aux_rows, rank), jnp.float32),
            pltpu.VMEM((2 * share, capacity * rank), jnp.bfloat16),
            pltpu.VMEM((4, capacity, 128), jnp.float32),
            dma((HALVES,)),
            dma((HALVES * 32,)),
            dma((HALVES * 2,)),
            dma((HALVES,)),
            dma((STEPS * 2,)),
            dma((STEPS,)),
            dma((STEPS * 4,)),
            dma((blocks,)),
            dma((blocks,)),
            dma((blocks,)),
        ],
        compiler_params=pltpu.CompilerParams(
            collective_id=0, has_side_effects=True, vmem_limit_bytes=60 * 2**20
        ),
    )(
        factors,
        pair_rows,
        aux_basis,
        aux_decay.reshape(aux_rows // 128, 128),
        item_pair,
        image_dist,
        image_phase,
        item_image,
        item_sub,
        item_count,
    )
    return result.reshape(result.shape[0], 2, rows)


def solution(mesh):
    return jax.shard_map(
        body,
        mesh=mesh,
        in_specs=(
            P("dev", None, "grp"),
            P("dev", None, "grp"),
            P("grp"),
            P(),
            P(),
            P(),
            P(),
            P(("grp", "dev"), None, None),
            P(("grp", "dev")),
            P(("grp", "dev")),
            P(("grp", "dev")),
        ),
        out_specs=P("grp", None, "dev"),
        check_vma=False,
    )
```

```python
import jax
import jax.numpy as jnp
from jax import lax
from jax.experimental import pallas as pl
from jax.experimental.pallas import tpu as pltpu
from jax.sharding import PartitionSpec as P

MESH = pl.DeviceIdType.MESH
HALVES = 2
SIDE = 4
STEPS = SIDE * HALVES
QUADS = ((0, 0, 0), (0, 2, 0), (0, 0, 1), (0, 2, 1), (2, 0, 0), (2, 2, 0), (2, 0, 1), (2, 2, 1))


def offset_of(index):
    high = index // 2
    return 2 * high + (high + index) % 2


def step_of(z_step, half):
    return z_step * HALVES + half


def wrap(value):
    return lax.rem(value + 8, 4)


def kernel(
    aux_ref,
    pair_ref,
    basis_ref,
    decay_ref,
    items_ref,
    dist_ref,
    phase_ref,
    image_ref,
    sub_ref,
    count_ref,
    out_ref,
    factors,
    total,
    chain_in,
    side_in,
    pair_in,
    reduce_out,
    long_lhs,
    short_lhs,
    basis_cols,
    damping,
    damped,
    scales,
    load_sem,
    factor_recv,
    z_send,
    z_relay,
    y_send,
    y_relay,
    core_send,
    reduce_send,
    chain_recv,
    side_recv,
    pair_recv,
):
    group, member = lax.axis_index("grp"), lax.axis_index("dev")
    z_low, x = lax.div(group, 4), lax.rem(group, 4)
    core, y, z = lax.rem(member, 2), lax.rem(lax.div(member, 2), 4), lax.div(member, 8)
    way = 1 - 2 * core
    piece = factors.shape[3]
    items = items_ref.shape[0]
    rank = items_ref.shape[1]
    columns = long_lhs.shape[0]
    side_rows = columns // 2
    depth = pair_ref.shape[1]
    half_k = depth // 2

    def place(z_at, y_at, core_at):
        return (group, (z_at * 4 + y_at) * 2 + core_at)

    def own_copy(half):
        return pltpu.make_async_copy(
            aux_ref.at[pl.ds(half * piece, piece)],
            factors.at[step_of(0, half), 0, core],
            load_sem.at[half],
        )

    for half in range(HALVES):
        own_copy(half).start()

    sibling = place(z, y, 1 - core)
    z_peers = (place(wrap(z + 1), y, core), place(wrap(z - 1), y, core))
    turn = 2 * lax.rem(y, 2) - 1
    y_peers = (place(z, wrap(y + turn), core), place(z, wrap(y - turn), core))
    y_ahead = place(z, wrap(y + way), core)
    x_down = (z_low * 4 + wrap(x - way), member)
    x_up = (z_low * 4 + wrap(x + way), member)
    z_pair = ((1 - z_low) * 4 + x, member)
    seen_as = (2, 1)

    peers = z_peers + y_peers + (sibling, x_down, x_up, z_pair)
    barrier = pltpu.get_barrier_semaphore()
    for peer in peers:
        pl.semaphore_signal(barrier, inc=1, device_id=peer, device_id_type=MESH)
    pl.semaphore_wait(barrier, len(peers))

    waits = []

    def factor_copy(source, sink, target, send_sem):
        step, row = sink
        return pltpu.make_async_remote_copy(
            src_ref=factors.at[source[0], source[1], core],
            dst_ref=factors.at[step, row, core],
            send_sem=send_sem,
            recv_sem=factor_recv.at[(step * 4 + row) * 2 + core],
            device_id=target,
            device_id_type=MESH,
        )

    def send(source, sink, target, send_sem):
        copy = factor_copy(source, sink, target, send_sem)
        copy.start()
        waits.append(copy)

    def await_factor(step, row, core_at):
        pltpu.make_async_remote_copy(
            src_ref=factors.at[step, row, core_at],
            dst_ref=factors.at[step, row, core_at],
            send_sem=load_sem.at[0],
            recv_sem=factor_recv.at[(step * 4 + row) * 2 + core_at],
            device_id=sibling,
            device_id_type=MESH,
        ).wait_recv()

    def relay_copy(z_step, half):
        step = step_of(z_step, half)
        return factor_copy(
            (step, 0), (step_of(3, half), 0), z_peers[2 - z_step], z_relay.at[half]
        )

    def send_column(z_step, half):
        step = step_of(z_step, half)
        if z_step == 0:
            own_copy(half).wait()
            for index, target in enumerate(z_peers):
                sink = (step_of(seen_as[index], half), 0)
                send((step, 0), sink, target, z_send.at[half * 2 + index])
        else:
            await_factor(step, 0, core)
            if z_step < 3:

                @pl.when(core == 2 - z_step)
                def _():
                    relay_copy(z_step, half).start()

        for index, target in enumerate(y_peers):
            send((step, 0), (step, index + 1), target, y_send.at[step * 2 + index])
        send((step, 0), (step, 0), sibling, core_send.at[step * 4])

    def send_rows(z_step, half):
        step = step_of(z_step, half)
        behind = 1 + lax.rem(core + y, 2)
        await_factor(step, behind, core)
        send((step, behind), (step, 3), y_ahead, y_relay.at[step])
        send((step, behind), (step, behind), sibling, core_send.at[step * 4 + 1])
        await_factor(step, 3 - behind, core)
        send((step, 3 - behind), (step, 3 - behind), sibling, core_send.at[step * 4 + 2])

    def send_far(z_step, half):
        step = step_of(z_step, half)
        await_factor(step, 3, core)
        send((step, 3), (step, 3), sibling, core_send.at[step * 4 + 3])

    def prepare():
        long_lhs[0:side_rows, :] = pair_ref[...]
        long_lhs[side_rows:columns, 0:half_k] = pair_ref[:, half_k:]
        long_lhs[side_rows:columns, half_k:] = -pair_ref[:, 0:half_k]

        slot = lax.broadcasted_iota(jnp.int32, (items, 128), 0)
        phases = jnp.zeros((items, 128), jnp.float32)
        reach = jnp.zeros((items, 128), jnp.float32)
        first = jnp.zeros((items, 128), jnp.float32)
        second = jnp.zeros((items, 128), jnp.float32)
        for index in range(items):
            alive = jnp.where(index < count_ref[0], 1.0, 0.0)
            to_second = sub_ref[index].astype(jnp.float32)
            phases = jnp.where(slot == index, phase_ref[image_ref[index]], phases)
            reach = jnp.where(slot == index, -dist_ref[image_ref[index]], reach)
            first = jnp.where(slot == index, alive * (1.0 - to_second), first)
            second = jnp.where(slot == index, alive * to_second, second)
        cosine, sine = jnp.cos(phases), jnp.sin(phases)
        scales[0] = cosine * first
        scales[1] = cosine * second
        scales[2] = sine * first
        scales[3] = sine * second

        def place_item(index, carry):
            block = items_ref[index].astype(jnp.float32).T
            at = pl.ds(pl.multiple_of(index * rank, rank), rank)
            for part in range(4):
                short_lhs[part * 128 : (part + 1) * 128, at] = (
                    block * scales[part, pl.ds(index, 1), :]
                ).astype(jnp.bfloat16)
            return carry

        lax.fori_loop(0, items, place_item, 0)

        def by_halves(left, right):
            low = lax.broadcasted_iota(jnp.int32, left.shape, 1) < piece
            return (
                jnp.where(low, left, pltpu.roll(right, piece, 1)),
                jnp.where(low, pltpu.roll(left, piece, 1), right),
            )

        def arrange(chip, carry):
            at = pl.multiple_of(chip * 256, 256)
            left, right = pl.ds(at, 128), pl.ds(at + 128, 128)
            basis_cols[:, left], basis_cols[:, right] = by_halves(
                basis_ref[:, left].astype(jnp.float32), basis_ref[:, right].astype(jnp.float32)
            )
            damping[:, left], damping[:, right] = by_halves(
                jnp.exp(reach * decay_ref[pl.ds(chip * 2, 1), :]),
                jnp.exp(reach * decay_ref[pl.ds(chip * 2 + 1, 1), :]),
            )
            return carry

        lax.fori_loop(0, basis_cols.shape[1] // 256, arrange, 0)

    def short_range(z_step):
        def one(y_step, carry):
            chip = wrap(z + offset_of(z_step)) * 4 + wrap(y + turn * offset_of(y_step))
            at = pl.ds(pl.multiple_of(chip * 256, 256), 256)
            for index in range(items):
                damped[index * rank : (index + 1) * rank, :] = (
                    basis_cols[:, at] * damping[index : index + 1, at]
                ).astype(jnp.bfloat16)
            product = jnp.dot(short_lhs[...], damped[...], preferred_element_type=jnp.float32)
            for half in range(HALVES):
                total[step_of(z_step, half) * 4 + y_step] = product[:, half * 128 : (half + 1) * 128]
            return carry

        lax.fori_loop(0, SIDE, one, 0)

    def roles(z_step, row):
        z_at = wrap(z + offset_of(z_step))
        y_at = wrap(y + turn * offset_of(row))
        x_at = lax.rem(z_at, 2) * 2 + lax.div(y_at, 2)
        role = wrap((x - x_at) * way)
        return role, lax.div(z_at, 2) == z_low, lax.rem(y_at, 2)

    def reduce_copy(block, sink, recv_sem, target):
        return pltpu.make_async_remote_copy(
            src_ref=reduce_out.at[block],
            dst_ref=sink.at[block],
            send_sem=reduce_send.at[block],
            recv_sem=recv_sem.at[block],
            device_id=target,
            device_id_type=MESH,
        )

    def chain_copy(block):
        return reduce_copy(block, chain_in, chain_recv, x_down)

    def side_copy(block):
        return reduce_copy(block, side_in, side_recv, x_up)

    def pair_copy(block):
        return reduce_copy(block, pair_in, pair_recv, z_pair)

    def long_range(quad):
        first_z, first_row, half = quad

        def one(pair, carry):
            z_step = first_z + pair
            step = step_of(z_step, half)
            for row in range(2):
                await_factor(step, first_row + row, 1 - core)
            rows = factors[step, first_row : first_row + 2].reshape(4 * piece, depth)
            product = lax.dot_general(
                long_lhs[...], rows, (((1,), (1,)), ((), ())), preferred_element_type=jnp.float32
            )
            for row in range(2):
                block = step * 4 + first_row + row
                total[block] += product[:, row * 128 : (row + 1) * 128]
                role, _, _ = roles(z_step, first_row + row)

                @pl.when(role >= 2)
                def _():
                    reduce_out[block] = total[block].astype(jnp.bfloat16)

                @pl.when(role == 2)
                def _():
                    chain_copy(block).start()

                @pl.when(role == 3)
                def _():
                    side_copy(block).start()

            return carry

        lax.fori_loop(0, 2, one, 0)

    def reduce_hop(quad, hop):
        first_z, first_row, half = quad

        def one(index, carry):
            z_step = first_z + index // 2
            row = first_row + index % 2
            block = step_of(z_step, half) * 4 + row
            role, keeps, odd_y = roles(z_step, row)
            if hop == 1:

                @pl.when(role == 1)
                def _():
                    chain_copy(block).wait_recv()
                    reduce_out[block] = (total[block] + chain_in[block].astype(jnp.float32)).astype(
                        jnp.bfloat16
                    )
                    chain_copy(block).start()

            elif hop == 2:

                @pl.when(role == 0)
                def _():
                    side_copy(block).wait_recv()
                    chain_copy(block).wait_recv()
                    total[block] += chain_in[block].astype(jnp.float32) + side_in[block].astype(
                        jnp.float32
                    )

                @pl.when((role == 0) & jnp.logical_not(keeps))
                def _():
                    reduce_out[block] = total[block].astype(jnp.bfloat16)
                    pair_copy(block).start()

            else:

                @pl.when((role == 0) & keeps)
                def _():
                    pair_copy(block).wait_recv()
                    done = (total[block] + pair_in[block].astype(jnp.float32)).T
                    for core_at in range(2):
                        start = odd_y * (4 * piece) + (core_at * HALVES + half) * piece
                        out_ref[pl.ds(pl.multiple_of(start, piece), piece), :] = done[
                            core_at * piece : (core_at + 1) * piece
                        ].astype(jnp.bfloat16)

            return carry

        lax.fori_loop(0, SIDE, one, 0)

    def advance(index):
        if index < len(QUADS):
            long_range(QUADS[index])
        for hop in (1, 2, 3):
            if 0 <= index - hop < len(QUADS):
                reduce_hop(QUADS[index - hop], hop)

    send_column(0, 0)
    send_column(0, 1)
    prepare()
    short_range(0)
    send_rows(0, 0)
    send_rows(0, 1)
    send_column(1, 0)
    send_column(2, 0)
    short_range(1)
    send_far(0, 0)
    send_rows(1, 0)
    send_far(0, 1)
    send_column(1, 1)
    advance(0)
    send_rows(2, 0)
    send_far(1, 0)
    send_column(3, 0)
    send_column(2, 1)
    advance(1)
    short_range(2)
    send_rows(1, 1)
    send_column(3, 1)
    advance(2)
    send_far(2, 0)
    send_far(1, 1)
    send_rows(3, 0)
    advance(3)
    short_range(3)
    send_rows(2, 1)
    advance(4)
    send_far(3, 0)
    send_rows(3, 1)
    advance(5)
    send_far(2, 1)
    advance(6)
    send_far(3, 1)
    for index in range(7, 11):
        advance(index)

    for copy in waits:
        copy.wait_send()
    for half in range(HALVES):
        relay_copy(1, half).wait_send()
    def drain(block, carry):
        role, keeps, _ = roles(block // (HALVES * SIDE), block % SIDE)

        @pl.when((role > 0) | jnp.logical_not(keeps))
        def _():
            chain_copy(block).wait_send()

        return carry

    lax.fori_loop(0, STEPS * SIDE, drain, 0)


def body(
    pair_ft,
    aux_ft,
    coul_weight,
    aux_basis,
    aux_decay,
    image_dist,
    image_phase,
    item_pair,
    item_image,
    item_sub,
    item_count,
):
    rows, _, depth = pair_ft.shape
    share = aux_ft.shape[0]
    aux_rows = aux_basis.shape[1]
    capacity, rank, _ = item_pair.shape
    columns = 2 * rows
    piece = share // HALVES
    weighted = (pair_ft.astype(jnp.float32) * coul_weight[None, None, :]).astype(jnp.bfloat16)
    pair_rows = weighted.reshape(rows, 2 * depth)
    factors = aux_ft.reshape(share, 2 * depth)
    blocks = STEPS * SIDE
    vmem = pl.BlockSpec(memory_space=pltpu.VMEM)
    smem = pl.BlockSpec(memory_space=pltpu.SMEM)
    dma = pltpu.SemaphoreType.DMA
    result = pl.pallas_call(
        kernel,
        out_shape=jax.ShapeDtypeStruct((aux_rows // lax.axis_size("grp"), columns), jnp.bfloat16),
        in_specs=[pl.BlockSpec(memory_space=pl.ANY)] + [vmem] * 4 + [smem] * 5,
        out_specs=vmem,
        scratch_shapes=[
            pltpu.VMEM((STEPS, SIDE, 2, piece, 2 * depth), jnp.bfloat16),
            pltpu.VMEM((blocks, columns, 2 * piece), jnp.float32),
            pltpu.VMEM((blocks, columns, 2 * piece), jnp.bfloat16),
            pltpu.VMEM((blocks, columns, 2 * piece), jnp.bfloat16),
            pltpu.VMEM((blocks, columns, 2 * piece), jnp.bfloat16),
            pltpu.VMEM((blocks, columns, 2 * piece), jnp.bfloat16),
            pltpu.VMEM((columns, 2 * depth), jnp.bfloat16),
            pltpu.VMEM((columns, capacity * rank), jnp.bfloat16),
            pltpu.VMEM((rank, aux_rows), jnp.float32),
            pltpu.VMEM((capacity, aux_rows), jnp.float32),
            pltpu.VMEM((capacity * rank, 2 * share), jnp.bfloat16),
            pltpu.VMEM((4, capacity, 128), jnp.float32),
            dma((HALVES,)),
            dma((blocks * 2,)),
            dma((HALVES * 2,)),
            dma((HALVES,)),
            dma((STEPS * 2,)),
            dma((STEPS,)),
            dma((blocks,)),
            dma((blocks,)),
            dma((blocks,)),
            dma((blocks,)),
            dma((blocks,)),
        ],
        compiler_params=pltpu.CompilerParams(
            collective_id=0, has_side_effects=True, vmem_limit_bytes=60 * 2**20
        ),
    )(
        factors,
        pair_rows,
        aux_basis,
        aux_decay.reshape(aux_rows // 128, 128),
        item_pair,
        image_dist,
        image_phase,
        item_image,
        item_sub,
        item_count,
    )
    return result.reshape(result.shape[0], 2, rows)


def solution(mesh):
    return jax.shard_map(
        body,
        mesh=mesh,
        in_specs=(
            P("dev", None, "grp"),
            P("dev", None, "grp"),
            P("grp"),
            P(),
            P(),
            P(),
            P(),
            P(("grp", "dev"), None, None),
            P(("grp", "dev")),
            P(("grp", "dev")),
            P(("grp", "dev")),
        ),
        out_specs=P("grp", None, "dev"),
        check_vma=False,
    )
```

```python
import jax
import jax.numpy as jnp
from jax import lax
from jax.experimental import pallas as pl
from jax.experimental.pallas import tpu as pltpu
from jax.sharding import PartitionSpec as P

MESH = pl.DeviceIdType.MESH
HALVES = 2
SIDE = 4
STEPS = SIDE * HALVES
QUADS = ((0, 0, 0), (0, 2, 0), (0, 0, 1), (0, 2, 1), (2, 0, 0), (2, 2, 0), (2, 0, 1), (2, 2, 1))


def offset_of(index):
    high = index // 2
    return 2 * high + (high + index) % 2
DIRECT = 0
LAGS = (1, 2, 3)


def step_of(z_step, half):
    return z_step * HALVES + half


def wrap(value):
    return lax.rem(value + 8, 4)


def kernel(
    aux_any,
    pair_any,
    basis_any,
    items_any,
    weight_ref,
    decay_ref,
    dist_ref,
    phase_ref,
    image_ref,
    sub_ref,
    count_ref,
    out_ref,
    factors,
    total,
    chain_in,
    side_in,
    far_in,
    pair_in,
    reduce_out,
    long_lhs,
    short_lhs,
    basis_cols,
    damping,
    damped,
    scales,
    aux_ref,
    pair_ref,
    basis_ref,
    items_ref,
    load_sem,
    factor_recv,
    z_send,
    z_relay,
    y_send,
    y_relay,
    core_send,
    reduce_send,
    chain_recv,
    side_recv,
    far_recv,
    pair_recv,
):
    group, member = lax.axis_index("grp"), lax.axis_index("dev")
    z_low, x = lax.div(group, 4), lax.rem(group, 4)
    core, y, z = lax.rem(member, 2), lax.rem(lax.div(member, 2), 4), lax.div(member, 8)
    way = 1 - 2 * core
    piece = factors.shape[3]
    items = items_ref.shape[0]
    rank = items_ref.shape[1]
    columns = long_lhs.shape[0]
    side_rows = columns // 2
    half_k = pair_ref.shape[2]
    depth = 2 * half_k

    def place(z_at, y_at, core_at):
        return (group, (z_at * 4 + y_at) * 2 + core_at)

    loads = [
        pltpu.make_async_copy(source, sink, load_sem.at[index])
        for index, (source, sink) in enumerate(
            ((aux_any, aux_ref), (items_any, items_ref), (basis_any, basis_ref), (pair_any, pair_ref))
        )
    ]
    for load in loads:
        load.start()

    sibling = place(z, y, 1 - core)
    z_peers = (place(wrap(z + 1), y, core), place(wrap(z - 1), y, core))
    turn = 2 * lax.rem(y, 2) - 1
    y_peers = (place(z, wrap(y + turn), core), place(z, wrap(y - turn), core))
    y_ahead = place(z, wrap(y + way), core)
    x_down = (z_low * 4 + wrap(x - way), member)
    x_up = (z_low * 4 + wrap(x + way), member)
    x_far = (z_low * 4 + wrap(x + 2), member)
    z_pair = ((1 - z_low) * 4 + x, member)
    seen_as = (2, 1)

    peers = z_peers + y_peers + (sibling, x_down, x_up, x_far, z_pair)
    barrier = pltpu.get_barrier_semaphore()
    for peer in peers:
        pl.semaphore_signal(barrier, inc=1, device_id=peer, device_id_type=MESH)
    loads[0].wait()
    for half in range(HALVES):
        own = aux_ref[half * piece : (half + 1) * piece]
        for part in range(2):
            factors[step_of(0, half), 0, core, :, part * half_k : (part + 1) * half_k] = own[:, part, :]
    pl.semaphore_wait(barrier, len(peers))

    waits = []

    def factor_copy(source, sink, target, send_sem):
        step, row = sink
        return pltpu.make_async_remote_copy(
            src_ref=factors.at[source[0], source[1], core],
            dst_ref=factors.at[step, row, core],
            send_sem=send_sem,
            recv_sem=factor_recv.at[(step * 4 + row) * 2 + core],
            device_id=target,
            device_id_type=MESH,
        )

    def send(source, sink, target, send_sem):
        copy = factor_copy(source, sink, target, send_sem)
        copy.start()
        waits.append(copy)

    def await_factor(step, row, core_at):
        pltpu.make_async_remote_copy(
            src_ref=factors.at[step, row, core_at],
            dst_ref=factors.at[step, row, core_at],
            send_sem=load_sem.at[0],
            recv_sem=factor_recv.at[(step * 4 + row) * 2 + core_at],
            device_id=sibling,
            device_id_type=MESH,
        ).wait_recv()

    def relay_copy(z_step, half):
        step = step_of(z_step, half)
        return factor_copy(
            (step, 0), (step_of(3, half), 0), z_peers[2 - z_step], z_relay.at[half]
        )

    def send_column(z_step, half):
        step = step_of(z_step, half)
        if z_step == 0:
            for index, target in enumerate(z_peers):
                sink = (step_of(seen_as[index], half), 0)
                send((step, 0), sink, target, z_send.at[half * 2 + index])
        else:
            await_factor(step, 0, core)
            if z_step < 3:

                @pl.when(core == 2 - z_step)
                def _():
                    relay_copy(z_step, half).start()

        for index, target in enumerate(y_peers):
            send((step, 0), (step, index + 1), target, y_send.at[step * 2 + index])
        send((step, 0), (step, 0), sibling, core_send.at[step * 4])

    def send_rows(z_step, half):
        step = step_of(z_step, half)
        behind = 1 + lax.rem(core + y, 2)
        await_factor(step, behind, core)
        send((step, behind), (step, 3), y_ahead, y_relay.at[step])
        send((step, behind), (step, behind), sibling, core_send.at[step * 4 + 1])
        await_factor(step, 3 - behind, core)
        send((step, 3 - behind), (step, 3 - behind), sibling, core_send.at[step * 4 + 2])

    def send_far(z_step, half):
        step = step_of(z_step, half)
        await_factor(step, 3, core)
        send((step, 3), (step, 3), sibling, core_send.at[step * 4 + 3])

    def prepare():
        loads[1].wait()

        slot = lax.broadcasted_iota(jnp.int32, (items, 128), 0)
        phases = jnp.zeros((items, 128), jnp.float32)
        reach = jnp.zeros((items, 128), jnp.float32)
        first = jnp.zeros((items, 128), jnp.float32)
        second = jnp.zeros((items, 128), jnp.float32)
        for index in range(items):
            alive = jnp.where(index < count_ref[0], 1.0, 0.0)
            to_second = sub_ref[index].astype(jnp.float32)
            phases = jnp.where(slot == index, phase_ref[image_ref[index]], phases)
            reach = jnp.where(slot == index, -dist_ref[image_ref[index]], reach)
            first = jnp.where(slot == index, alive * (1.0 - to_second), first)
            second = jnp.where(slot == index, alive * to_second, second)
        cosine, sine = jnp.cos(phases), jnp.sin(phases)
        scales[0] = cosine * first
        scales[1] = cosine * second
        scales[2] = sine * first
        scales[3] = sine * second

        def place_item(index, carry):
            block = items_ref[index].astype(jnp.float32).T
            at = pl.ds(pl.multiple_of(index * rank, rank), rank)
            for part in range(4):
                short_lhs[part * 128 : (part + 1) * 128, at] = (
                    block * scales[part, pl.ds(index, 1), :]
                ).astype(jnp.bfloat16)
            return carry

        lax.fori_loop(0, items, place_item, 0)

        loads[2].wait()

        def by_halves(left, right):
            low = lax.broadcasted_iota(jnp.int32, left.shape, 1) < piece
            return (
                jnp.where(low, left, pltpu.roll(right, piece, 1)),
                jnp.where(low, pltpu.roll(left, piece, 1), right),
            )

        def arrange(chip, carry):
            at = pl.multiple_of(chip * 256, 256)
            left, right = pl.ds(at, 128), pl.ds(at + 128, 128)
            basis_cols[:, left], basis_cols[:, right] = by_halves(
                basis_ref[:, left].astype(jnp.float32), basis_ref[:, right].astype(jnp.float32)
            )
            damping[:, left], damping[:, right] = by_halves(
                jnp.exp(reach * decay_ref[pl.ds(chip * 2, 1), :]),
                jnp.exp(reach * decay_ref[pl.ds(chip * 2 + 1, 1), :]),
            )
            return carry

        lax.fori_loop(0, basis_cols.shape[1] // 256, arrange, 0)

    def weigh():
        loads[3].wait()

        def rows_of(index, carry):
            at = pl.ds(pl.multiple_of(index * 32, 32), 32)
            low = pl.ds(pl.multiple_of(side_rows + index * 32, 32), 32)
            scaled = (pair_ref[at].astype(jnp.float32) * weight_ref[...][None]).astype(jnp.bfloat16)
            real_part, imag_part = scaled[:, 0, :], scaled[:, 1, :]
            long_lhs[at, 0:half_k] = real_part
            long_lhs[at, half_k:] = imag_part
            long_lhs[low, 0:half_k] = imag_part
            long_lhs[low, half_k:] = -real_part
            return carry

        lax.fori_loop(0, side_rows // 32, rows_of, 0)

    def short_range(z_step):
        def one(y_step, carry):
            chip = wrap(z + offset_of(z_step)) * 4 + wrap(y + turn * offset_of(y_step))
            at = pl.ds(pl.multiple_of(chip * 256, 256), 256)
            for index in range(items):
                damped[index * rank : (index + 1) * rank, :] = (
                    basis_cols[:, at] * damping[index : index + 1, at]
                ).astype(jnp.bfloat16)
            product = jnp.dot(short_lhs[...], damped[...], preferred_element_type=jnp.float32)
            for half in range(HALVES):
                total[step_of(z_step, half) * 4 + y_step] = product[:, half * 128 : (half + 1) * 128]
            return carry

        lax.fori_loop(0, SIDE, one, 0)

    def roles(z_step, row):
        z_at = wrap(z + offset_of(z_step))
        y_at = wrap(y + turn * offset_of(row))
        x_at = lax.rem(z_at, 2) * 2 + lax.div(y_at, 2)
        role = wrap((x - x_at) * way)
        return role, lax.div(z_at, 2) == z_low, lax.rem(y_at, 2)

    def reduce_copy(block, sink, recv_sem, target):
        return pltpu.make_async_remote_copy(
            src_ref=reduce_out.at[block],
            dst_ref=sink.at[block],
            send_sem=reduce_send.at[block],
            recv_sem=recv_sem.at[block],
            device_id=target,
            device_id_type=MESH,
        )

    def chain_copy(block):
        return reduce_copy(block, chain_in, chain_recv, x_down)

    def side_copy(block):
        return reduce_copy(block, side_in, side_recv, x_up)

    def far_copy(block):
        return reduce_copy(block, far_in, far_recv, x_far)

    def pair_copy(block):
        return reduce_copy(block, pair_in, pair_recv, z_pair)

    def long_range(quad):
        first_z, first_row, half = quad

        def one(pair, carry):
            z_step = first_z + pair
            step = step_of(z_step, half)
            for row in range(2):
                await_factor(step, first_row + row, 1 - core)
            rows = factors[step, first_row : first_row + 2].reshape(4 * piece, depth)
            product = lax.dot_general(
                long_lhs[...], rows, (((1,), (1,)), ((), ())), preferred_element_type=jnp.float32
            )
            for row in range(2):
                block = step * 4 + first_row + row
                total[block] += product[:, row * 128 : (row + 1) * 128]
                role, _, _ = roles(z_step, first_row + row)

                direct = quad in QUADS[len(QUADS) - DIRECT :]

                @pl.when(role >= (1 if direct else 2))
                def _():
                    reduce_out[block] = total[block].astype(jnp.bfloat16)

                @pl.when(role == (1 if direct else 2))
                def _():
                    chain_copy(block).start()

                if direct:

                    @pl.when(role == 2)
                    def _():
                        far_copy(block).start()

                @pl.when(role == 3)
                def _():
                    side_copy(block).start()

            return carry

        lax.fori_loop(0, 2, one, 0)

    def reduce_hop(quad, hop):
        first_z, first_row, half = quad
        direct = quad in QUADS[len(QUADS) - DIRECT :]
        if direct and hop == 1:
            return

        def one(index, carry):
            z_step = first_z + index // 2
            row = first_row + index % 2
            block = step_of(z_step, half) * 4 + row
            role, keeps, odd_y = roles(z_step, row)
            if hop == 1:

                @pl.when(role == 1)
                def _():
                    chain_copy(block).wait_recv()
                    reduce_out[block] = (total[block] + chain_in[block].astype(jnp.float32)).astype(
                        jnp.bfloat16
                    )
                    chain_copy(block).start()

            elif hop == 2:

                @pl.when(role == 0)
                def _():
                    side_copy(block).wait_recv()
                    chain_copy(block).wait_recv()
                    others = chain_in[block].astype(jnp.float32) + side_in[block].astype(jnp.float32)
                    if direct:
                        far_copy(block).wait_recv()
                        others += far_in[block].astype(jnp.float32)
                    total[block] += others

                @pl.when((role == 0) & jnp.logical_not(keeps))
                def _():
                    reduce_out[block] = total[block].astype(jnp.bfloat16)
                    pair_copy(block).start()

            else:

                @pl.when((role == 0) & keeps)
                def _():
                    pair_copy(block).wait_recv()
                    done = (total[block] + pair_in[block].astype(jnp.float32)).T
                    for core_at in range(2):
                        start = odd_y * (4 * piece) + (core_at * HALVES + half) * piece
                        out_ref[pl.ds(pl.multiple_of(start, piece), piece), :] = done[
                            core_at * piece : (core_at + 1) * piece
                        ].astype(jnp.bfloat16)

            return carry

        lax.fori_loop(0, SIDE, one, 0)

    def advance(index):
        if index < len(QUADS):
            long_range(QUADS[index])
        for hop, lag in zip((1, 2, 3), LAGS):
            if 0 <= index - lag < len(QUADS):
                reduce_hop(QUADS[index - lag], hop)

    send_column(0, 0)
    send_column(0, 1)
    prepare()
    short_range(0)
    send_rows(0, 0)
    send_rows(0, 1)
    send_column(1, 0)
    send_column(2, 0)
    weigh()
    short_range(1)
    send_far(0, 0)
    send_rows(1, 0)
    send_far(0, 1)
    send_column(1, 1)
    advance(0)
    send_rows(2, 0)
    send_far(1, 0)
    send_column(3, 0)
    send_column(2, 1)
    advance(1)
    short_range(2)
    send_rows(1, 1)
    send_column(3, 1)
    advance(2)
    send_far(2, 0)
    send_far(1, 1)
    send_rows(3, 0)
    advance(3)
    short_range(3)
    send_rows(2, 1)
    advance(4)
    send_far(3, 0)
    send_rows(3, 1)
    advance(5)
    send_far(2, 1)
    advance(6)
    send_far(3, 1)
    def drain(block, carry):
        role, keeps, _ = roles(block // (HALVES * SIDE), block % SIDE)

        @pl.when((role > 0) | jnp.logical_not(keeps))
        def _():
            chain_copy(block).wait_send()

        return carry

    advance(7)
    for copy in waits:
        copy.wait_send()
    for half in range(HALVES):
        relay_copy(1, half).wait_send()
    for index in range(8, len(QUADS) + LAGS[2]):
        advance(index)
        if index == 8:
            lax.fori_loop(0, STEPS * SIDE // 2, drain, 0)
    lax.fori_loop(STEPS * SIDE // 2, STEPS * SIDE, drain, 0)


def body(
    pair_ft,
    aux_ft,
    coul_weight,
    aux_basis,
    aux_decay,
    image_dist,
    image_phase,
    item_pair,
    item_image,
    item_sub,
    item_count,
):
    rows, _, depth = pair_ft.shape
    share = aux_ft.shape[0]
    aux_rows = aux_basis.shape[1]
    capacity, rank, _ = item_pair.shape
    columns = 2 * rows
    piece = share // HALVES
    blocks = STEPS * SIDE
    vmem = pl.BlockSpec(memory_space=pltpu.VMEM)
    smem = pl.BlockSpec(memory_space=pltpu.SMEM)
    dma = pltpu.SemaphoreType.DMA
    result = pl.pallas_call(
        kernel,
        out_shape=jax.ShapeDtypeStruct((aux_rows // lax.axis_size("grp"), columns), jnp.bfloat16),
        in_specs=[pl.BlockSpec(memory_space=pl.ANY)] * 4 + [vmem] * 2 + [smem] * 5,
        out_specs=vmem,
        scratch_shapes=[
            pltpu.VMEM((STEPS, SIDE, 2, piece, 2 * depth), jnp.bfloat16),
            pltpu.VMEM((blocks, columns, 2 * piece), jnp.float32),
            pltpu.VMEM((blocks, columns, 2 * piece), jnp.bfloat16),
            pltpu.VMEM((blocks, columns, 2 * piece), jnp.bfloat16),
            pltpu.VMEM((blocks, columns, 2 * piece), jnp.bfloat16),
            pltpu.VMEM((blocks, columns, 2 * piece), jnp.bfloat16),
            pltpu.VMEM((blocks, columns, 2 * piece), jnp.bfloat16),
            pltpu.VMEM((columns, 2 * depth), jnp.bfloat16),
            pltpu.VMEM((columns, capacity * rank), jnp.bfloat16),
            pltpu.VMEM((rank, aux_rows), jnp.float32),
            pltpu.VMEM((capacity, aux_rows), jnp.float32),
            pltpu.VMEM((capacity * rank, 2 * share), jnp.bfloat16),
            pltpu.VMEM((4, capacity, 128), jnp.float32),
            pltpu.VMEM((share, 2, depth), jnp.bfloat16),
            pltpu.VMEM((rows, 2, depth), jnp.bfloat16),
            pltpu.VMEM((rank, aux_rows), jnp.bfloat16),
            pltpu.VMEM((capacity, rank, 128), jnp.bfloat16),
            dma((4,)),
            dma((blocks * 2,)),
            dma((HALVES * 2,)),
            dma((HALVES,)),
            dma((STEPS * 2,)),
            dma((STEPS,)),
            dma((blocks,)),
            dma((blocks,)),
            dma((blocks,)),
            dma((blocks,)),
            dma((blocks,)),
            dma((blocks,)),
        ],
        compiler_params=pltpu.CompilerParams(
            collective_id=0, has_side_effects=True, vmem_limit_bytes=60 * 2**20
        ),
    )(
        aux_ft,
        pair_ft,
        aux_basis,
        item_pair,
        coul_weight.reshape(1, depth),
        aux_decay.reshape(aux_rows // 128, 128),
        image_dist,
        image_phase,
        item_image,
        item_sub,
        item_count,
    )
    return result.reshape(result.shape[0], 2, rows)


def solution(mesh):
    return jax.shard_map(
        body,
        mesh=mesh,
        in_specs=(
            P("dev", None, "grp"),
            P("dev", None, "grp"),
            P("grp"),
            P(),
            P(),
            P(),
            P(),
            P(("grp", "dev"), None, None),
            P(("grp", "dev")),
            P(("grp", "dev")),
            P(("grp", "dev")),
        ),
        out_specs=P("grp", None, "dev"),
        check_vma=False,
    )
```

```python
import jax
import jax.numpy as jnp
from jax import lax
from jax.experimental import pallas as pl
from jax.experimental.pallas import tpu as pltpu
from jax.sharding import PartitionSpec as P

MESH = pl.DeviceIdType.MESH
HALVES = 2
SIDE = 4
STEPS = SIDE * HALVES
QUADS = ((0, 0, 0), (0, 2, 0), (0, 0, 1), (0, 2, 1), (2, 0, 0), (2, 2, 0), (2, 0, 1), (2, 2, 1))


def offset_of(index):
    high = index // 2
    return 2 * high + (high + index) % 2
DIRECT = 0
LAGS = (1, 3, 4)


def step_of(z_step, half):
    return z_step * HALVES + half


def wrap(value):
    return lax.rem(value + 8, 4)


def kernel(
    aux_any,
    pair_any,
    basis_any,
    items_any,
    weight_ref,
    decay_ref,
    dist_ref,
    phase_ref,
    image_ref,
    sub_ref,
    count_ref,
    out_ref,
    factors,
    total,
    chain_in,
    side_in,
    far_in,
    pair_in,
    reduce_out,
    long_lhs,
    short_lhs,
    basis_cols,
    damping,
    damped,
    scales,
    aux_ref,
    pair_ref,
    basis_ref,
    items_ref,
    load_sem,
    factor_recv,
    z_send,
    z_relay,
    y_send,
    y_relay,
    core_send,
    reduce_send,
    chain_recv,
    side_recv,
    far_recv,
    pair_recv,
):
    group, member = lax.axis_index("grp"), lax.axis_index("dev")
    z_low, x = lax.div(group, 4), lax.rem(group, 4)
    core, y, z = lax.rem(member, 2), lax.rem(lax.div(member, 2), 4), lax.div(member, 8)
    way = 1 - 2 * core
    piece = factors.shape[3]
    items = items_ref.shape[0]
    rank = items_ref.shape[1]
    columns = long_lhs.shape[0]
    side_rows = columns // 2
    half_k = pair_ref.shape[2]
    depth = 2 * half_k

    def place(z_at, y_at, core_at):
        return (group, (z_at * 4 + y_at) * 2 + core_at)

    loads = [
        pltpu.make_async_copy(source, sink, load_sem.at[index])
        for index, (source, sink) in enumerate(
            ((aux_any, aux_ref), (items_any, items_ref), (basis_any, basis_ref), (pair_any, pair_ref))
        )
    ]
    for load in loads:
        load.start()

    sibling = place(z, y, 1 - core)
    z_peers = (place(wrap(z + 1), y, core), place(wrap(z - 1), y, core))
    turn = 2 * lax.rem(y, 2) - 1
    y_peers = (place(z, wrap(y + turn), core), place(z, wrap(y - turn), core))
    y_ahead = place(z, wrap(y + way), core)
    x_down = (z_low * 4 + wrap(x - way), member)
    x_up = (z_low * 4 + wrap(x + way), member)
    x_far = (z_low * 4 + wrap(x + 2), member)
    z_pair = ((1 - z_low) * 4 + x, member)
    seen_as = (2, 1)

    peers = z_peers + y_peers + (sibling, x_down, x_up, x_far, z_pair)
    barrier = pltpu.get_barrier_semaphore()
    for peer in peers:
        pl.semaphore_signal(barrier, inc=1, device_id=peer, device_id_type=MESH)
    loads[0].wait()
    for half in range(HALVES):
        own = aux_ref[half * piece : (half + 1) * piece]
        for part in range(2):
            factors[step_of(0, half), 0, core, :, part * half_k : (part + 1) * half_k] = own[:, part, :]
    pl.semaphore_wait(barrier, len(peers))

    waits = []

    def factor_copy(source, sink, target, send_sem):
        step, row = sink
        return pltpu.make_async_remote_copy(
            src_ref=factors.at[source[0], source[1], core],
            dst_ref=factors.at[step, row, core],
            send_sem=send_sem,
            recv_sem=factor_recv.at[(step * 4 + row) * 2 + core],
            device_id=target,
            device_id_type=MESH,
        )

    def send(source, sink, target, send_sem):
        copy = factor_copy(source, sink, target, send_sem)
        copy.start()
        waits.append(copy)

    def await_factor(step, row, core_at):
        pltpu.make_async_remote_copy(
            src_ref=factors.at[step, row, core_at],
            dst_ref=factors.at[step, row, core_at],
            send_sem=load_sem.at[0],
            recv_sem=factor_recv.at[(step * 4 + row) * 2 + core_at],
            device_id=sibling,
            device_id_type=MESH,
        ).wait_recv()

    def relay_copy(z_step, half):
        step = step_of(z_step, half)
        return factor_copy(
            (step, 0), (step_of(3, half), 0), z_peers[2 - z_step], z_relay.at[half]
        )

    def send_column(z_step, half):
        step = step_of(z_step, half)
        if z_step == 0:
            for index, target in enumerate(z_peers):
                sink = (step_of(seen_as[index], half), 0)
                send((step, 0), sink, target, z_send.at[half * 2 + index])
        else:
            await_factor(step, 0, core)
            if z_step < 3:

                @pl.when(core == 2 - z_step)
                def _():
                    relay_copy(z_step, half).start()

        for index, target in enumerate(y_peers):
            send((step, 0), (step, index + 1), target, y_send.at[step * 2 + index])
        send((step, 0), (step, 0), sibling, core_send.at[step * 4])

    def send_rows(z_step, half):
        step = step_of(z_step, half)
        behind = 1 + lax.rem(core + y, 2)
        await_factor(step, behind, core)
        send((step, behind), (step, 3), y_ahead, y_relay.at[step])
        send((step, behind), (step, behind), sibling, core_send.at[step * 4 + 1])
        await_factor(step, 3 - behind, core)
        send((step, 3 - behind), (step, 3 - behind), sibling, core_send.at[step * 4 + 2])

    def send_far(z_step, half):
        step = step_of(z_step, half)
        await_factor(step, 3, core)
        send((step, 3), (step, 3), sibling, core_send.at[step * 4 + 3])

    def prepare():
        loads[1].wait()

        slot = lax.broadcasted_iota(jnp.int32, (items, 128), 0)
        phases = jnp.zeros((items, 128), jnp.float32)
        reach = jnp.zeros((items, 128), jnp.float32)
        first = jnp.zeros((items, 128), jnp.float32)
        second = jnp.zeros((items, 128), jnp.float32)
        for index in range(items):
            alive = jnp.where(index < count_ref[0], 1.0, 0.0)
            to_second = sub_ref[index].astype(jnp.float32)
            phases = jnp.where(slot == index, phase_ref[image_ref[index]], phases)
            reach = jnp.where(slot == index, -dist_ref[image_ref[index]], reach)
            first = jnp.where(slot == index, alive * (1.0 - to_second), first)
            second = jnp.where(slot == index, alive * to_second, second)
        cosine, sine = jnp.cos(phases), jnp.sin(phases)
        scales[0] = cosine * first
        scales[1] = cosine * second
        scales[2] = sine * first
        scales[3] = sine * second

        def place_item(index, carry):
            block = items_ref[index].astype(jnp.float32).T
            at = pl.ds(pl.multiple_of(index * rank, rank), rank)
            for part in range(4):
                short_lhs[part * 128 : (part + 1) * 128, at] = (
                    block * scales[part, pl.ds(index, 1), :]
                ).astype(jnp.bfloat16)
            return carry

        lax.fori_loop(0, items, place_item, 0)

        loads[2].wait()

        def by_halves(left, right):
            low = lax.broadcasted_iota(jnp.int32, left.shape, 1) < piece
            return (
                jnp.where(low, left, pltpu.roll(right, piece, 1)),
                jnp.where(low, pltpu.roll(left, piece, 1), right),
            )

        def arrange(chip, carry):
            at = pl.multiple_of(chip * 256, 256)
            left, right = pl.ds(at, 128), pl.ds(at + 128, 128)
            basis_cols[:, left], basis_cols[:, right] = by_halves(
                basis_ref[:, left].astype(jnp.float32), basis_ref[:, right].astype(jnp.float32)
            )
            damping[:, left], damping[:, right] = by_halves(
                jnp.exp(reach * decay_ref[pl.ds(chip * 2, 1), :]),
                jnp.exp(reach * decay_ref[pl.ds(chip * 2 + 1, 1), :]),
            )
            return carry

        lax.fori_loop(0, basis_cols.shape[1] // 256, arrange, 0)

    def weigh():
        loads[3].wait()

        def rows_of(index, carry):
            at = pl.ds(pl.multiple_of(index * 32, 32), 32)
            low = pl.ds(pl.multiple_of(side_rows + index * 32, 32), 32)
            scaled = (pair_ref[at].astype(jnp.float32) * weight_ref[...][None]).astype(jnp.bfloat16)
            real_part, imag_part = scaled[:, 0, :], scaled[:, 1, :]
            long_lhs[at, 0:half_k] = real_part
            long_lhs[at, half_k:] = imag_part
            long_lhs[low, 0:half_k] = imag_part
            long_lhs[low, half_k:] = -real_part
            return carry

        lax.fori_loop(0, side_rows // 32, rows_of, 0)

    def short_range(z_step):
        def one(y_step, carry):
            chip = wrap(z + offset_of(z_step)) * 4 + wrap(y + turn * offset_of(y_step))
            at = pl.ds(pl.multiple_of(chip * 256, 256), 256)
            for index in range(items):
                damped[index * rank : (index + 1) * rank, :] = (
                    basis_cols[:, at] * damping[index : index + 1, at]
                ).astype(jnp.bfloat16)
            product = jnp.dot(short_lhs[...], damped[...], preferred_element_type=jnp.float32)
            for half in range(HALVES):
                total[step_of(z_step, half) * 4 + y_step] = product[:, half * 128 : (half + 1) * 128]
            return carry

        lax.fori_loop(0, SIDE, one, 0)

    def roles(z_step, row):
        z_at = wrap(z + offset_of(z_step))
        y_at = wrap(y + turn * offset_of(row))
        x_at = lax.rem(z_at, 2) * 2 + lax.div(y_at, 2)
        role = wrap((x - x_at) * way)
        return role, lax.div(z_at, 2) == z_low, lax.rem(y_at, 2)

    def reduce_copy(block, sink, recv_sem, target):
        return pltpu.make_async_remote_copy(
            src_ref=reduce_out.at[block],
            dst_ref=sink.at[block],
            send_sem=reduce_send.at[block],
            recv_sem=recv_sem.at[block],
            device_id=target,
            device_id_type=MESH,
        )

    def chain_copy(block):
        return reduce_copy(block, chain_in, chain_recv, x_down)

    def side_copy(block):
        return reduce_copy(block, side_in, side_recv, x_up)

    def far_copy(block):
        return reduce_copy(block, far_in, far_recv, x_far)

    def pair_copy(block):
        return reduce_copy(block, pair_in, pair_recv, z_pair)

    def long_range(quad):
        first_z, first_row, half = quad

        def one(pair, carry):
            z_step = first_z + pair
            step = step_of(z_step, half)
            for row in range(2):
                await_factor(step, first_row + row, 1 - core)
            rows = factors[step, first_row : first_row + 2].reshape(4 * piece, depth)
            product = lax.dot_general(
                long_lhs[...], rows, (((1,), (1,)), ((), ())), preferred_element_type=jnp.float32
            )
            for row in range(2):
                block = step * 4 + first_row + row
                total[block] += product[:, row * 128 : (row + 1) * 128]
                role, _, _ = roles(z_step, first_row + row)

                direct = quad in QUADS[len(QUADS) - DIRECT :]

                @pl.when(role >= (1 if direct else 2))
                def _():
                    reduce_out[block] = total[block].astype(jnp.bfloat16)

                @pl.when(role == (1 if direct else 2))
                def _():
                    chain_copy(block).start()

                if direct:

                    @pl.when(role == 2)
                    def _():
                        far_copy(block).start()

                @pl.when(role == 3)
                def _():
                    side_copy(block).start()

            return carry

        lax.fori_loop(0, 2, one, 0)

    def reduce_hop(quad, hop):
        first_z, first_row, half = quad
        direct = quad in QUADS[len(QUADS) - DIRECT :]
        if direct and hop == 1:
            return

        def one(index, carry):
            z_step = first_z + index // 2
            row = first_row + index % 2
            block = step_of(z_step, half) * 4 + row
            role, keeps, odd_y = roles(z_step, row)
            if hop == 1:

                @pl.when(role == 1)
                def _():
                    chain_copy(block).wait_recv()
                    reduce_out[block] = (total[block] + chain_in[block].astype(jnp.float32)).astype(
                        jnp.bfloat16
                    )
                    chain_copy(block).start()

            elif hop == 2:

                @pl.when(role == 0)
                def _():
                    side_copy(block).wait_recv()
                    chain_copy(block).wait_recv()
                    others = chain_in[block].astype(jnp.float32) + side_in[block].astype(jnp.float32)
                    if direct:
                        far_copy(block).wait_recv()
                        others += far_in[block].astype(jnp.float32)
                    total[block] += others

                @pl.when((role == 0) & jnp.logical_not(keeps))
                def _():
                    reduce_out[block] = total[block].astype(jnp.bfloat16)
                    pair_copy(block).start()

            else:

                @pl.when((role == 0) & keeps)
                def _():
                    pair_copy(block).wait_recv()
                    done = (total[block] + pair_in[block].astype(jnp.float32)).T
                    for core_at in range(2):
                        start = odd_y * (4 * piece) + (core_at * HALVES + half) * piece
                        out_ref[pl.ds(pl.multiple_of(start, piece), piece), :] = done[
                            core_at * piece : (core_at + 1) * piece
                        ].astype(jnp.bfloat16)

            return carry

        lax.fori_loop(0, SIDE, one, 0)

    def advance(index):
        def hop_of(hop):
            at = index - LAGS[hop - 1]
            if 0 <= at < len(QUADS):
                reduce_hop(QUADS[at], hop)

        hop_of(2)
        hop_of(3)
        if index < len(QUADS):
            long_range(QUADS[index])
        hop_of(1)

    send_column(0, 0)
    send_column(0, 1)
    prepare()
    short_range(0)
    send_rows(0, 0)
    send_rows(0, 1)
    send_column(1, 0)
    send_column(2, 0)
    weigh()
    short_range(1)
    send_far(0, 0)
    send_rows(1, 0)
    send_far(0, 1)
    send_column(1, 1)
    short_range(2)
    advance(0)
    send_rows(2, 0)
    send_far(1, 0)
    send_column(3, 0)
    send_column(2, 1)
    advance(1)
    send_rows(1, 1)
    send_column(3, 1)
    advance(2)
    send_far(2, 0)
    send_far(1, 1)
    send_rows(3, 0)
    advance(3)
    short_range(3)
    send_rows(2, 1)
    advance(4)
    send_far(3, 0)
    advance(5)
    send_rows(3, 1)
    send_far(2, 1)
    advance(6)
    send_far(3, 1)
    def drain(block, carry):
        role, keeps, _ = roles(block // (HALVES * SIDE), block % SIDE)

        @pl.when((role > 0) | jnp.logical_not(keeps))
        def _():
            chain_copy(block).wait_send()

        return carry

    advance(7)
    for copy in waits:
        copy.wait_send()
    for half in range(HALVES):
        relay_copy(1, half).wait_send()
    for index in range(8, len(QUADS) + LAGS[2]):
        advance(index)
        if index == 8:
            lax.fori_loop(0, STEPS * SIDE // 2, drain, 0)
    lax.fori_loop(STEPS * SIDE // 2, STEPS * SIDE, drain, 0)


def body(
    pair_ft,
    aux_ft,
    coul_weight,
    aux_basis,
    aux_decay,
    image_dist,
    image_phase,
    item_pair,
    item_image,
    item_sub,
    item_count,
):
    rows, _, depth = pair_ft.shape
    share = aux_ft.shape[0]
    aux_rows = aux_basis.shape[1]
    capacity, rank, _ = item_pair.shape
    columns = 2 * rows
    piece = share // HALVES
    blocks = STEPS * SIDE
    vmem = pl.BlockSpec(memory_space=pltpu.VMEM)
    smem = pl.BlockSpec(memory_space=pltpu.SMEM)
    dma = pltpu.SemaphoreType.DMA
    result = pl.pallas_call(
        kernel,
        out_shape=jax.ShapeDtypeStruct((aux_rows // lax.axis_size("grp"), columns), jnp.bfloat16),
        in_specs=[pl.BlockSpec(memory_space=pl.ANY)] * 4 + [vmem] * 2 + [smem] * 5,
        out_specs=vmem,
        scratch_shapes=[
            pltpu.VMEM((STEPS, SIDE, 2, piece, 2 * depth), jnp.bfloat16),
            pltpu.VMEM((blocks, columns, 2 * piece), jnp.float32),
            pltpu.VMEM((blocks, columns, 2 * piece), jnp.bfloat16),
            pltpu.VMEM((blocks, columns, 2 * piece), jnp.bfloat16),
            pltpu.VMEM((blocks, columns, 2 * piece), jnp.bfloat16),
            pltpu.VMEM((blocks, columns, 2 * piece), jnp.bfloat16),
            pltpu.VMEM((blocks, columns, 2 * piece), jnp.bfloat16),
            pltpu.VMEM((columns, 2 * depth), jnp.bfloat16),
            pltpu.VMEM((columns, capacity * rank), jnp.bfloat16),
            pltpu.VMEM((rank, aux_rows), jnp.float32),
            pltpu.VMEM((capacity, aux_rows), jnp.float32),
            pltpu.VMEM((capacity * rank, 2 * share), jnp.bfloat16),
            pltpu.VMEM((4, capacity, 128), jnp.float32),
            pltpu.VMEM((share, 2, depth), jnp.bfloat16),
            pltpu.VMEM((rows, 2, depth), jnp.bfloat16),
            pltpu.VMEM((rank, aux_rows), jnp.bfloat16),
            pltpu.VMEM((capacity, rank, 128), jnp.bfloat16),
            dma((4,)),
            dma((blocks * 2,)),
            dma((HALVES * 2,)),
            dma((HALVES,)),
            dma((STEPS * 2,)),
            dma((STEPS,)),
            dma((blocks,)),
            dma((blocks,)),
            dma((blocks,)),
            dma((blocks,)),
            dma((blocks,)),
            dma((blocks,)),
        ],
        compiler_params=pltpu.CompilerParams(
            collective_id=0, has_side_effects=True, vmem_limit_bytes=60 * 2**20
        ),
    )(
        aux_ft,
        pair_ft,
        aux_basis,
        item_pair,
        coul_weight.reshape(1, depth),
        aux_decay.reshape(aux_rows // 128, 128),
        image_dist,
        image_phase,
        item_image,
        item_sub,
        item_count,
    )
    return result.reshape(result.shape[0], 2, rows)


def solution(mesh):
    return jax.shard_map(
        body,
        mesh=mesh,
        in_specs=(
            P("dev", None, "grp"),
            P("dev", None, "grp"),
            P("grp"),
            P(),
            P(),
            P(),
            P(),
            P(("grp", "dev"), None, None),
            P(("grp", "dev")),
            P(("grp", "dev")),
            P(("grp", "dev")),
        ),
        out_specs=P("grp", None, "dev"),
        check_vma=False,
    )
```

```python
import jax
import jax.numpy as jnp
from jax import lax
from jax.experimental import pallas as pl
from jax.experimental.pallas import tpu as pltpu
from jax.sharding import PartitionSpec as P

MESH = pl.DeviceIdType.MESH
HALVES = 2
SIDE = 4
STEPS = SIDE * HALVES
QUADS = ((0, 0, 0), (0, 2, 0), (0, 0, 1), (0, 2, 1), (2, 0, 0), (2, 2, 0), (2, 0, 1), (2, 2, 1))


def offset_of(index):
    high = index // 2
    return 2 * high + (high + index) % 2
DIRECT = 0
LAGS = (1, 3, 4)


def step_of(z_step, half):
    return z_step * HALVES + half


def wrap(value):
    return lax.rem(value + 8, 4)


def kernel(
    aux_any,
    pair_any,
    basis_any,
    items_any,
    weight_ref,
    decay_ref,
    dist_ref,
    phase_ref,
    image_ref,
    sub_ref,
    count_ref,
    out_ref,
    factors,
    total,
    chain_in,
    side_in,
    far_in,
    pair_in,
    reduce_out,
    long_lhs,
    short_lhs,
    basis_cols,
    damping,
    damped,
    scales,
    aux_ref,
    pair_ref,
    basis_ref,
    items_ref,
    load_sem,
    factor_recv,
    z_send,
    z_relay,
    y_send,
    y_relay,
    core_send,
    reduce_send,
    chain_recv,
    side_recv,
    far_recv,
    pair_recv,
):
    group, member = lax.axis_index("grp"), lax.axis_index("dev")
    z_low, x = lax.div(group, 4), lax.rem(group, 4)
    core, y, z = lax.rem(member, 2), lax.rem(lax.div(member, 2), 4), lax.div(member, 8)
    way = 1 - 2 * core
    piece = factors.shape[3]
    items = items_ref.shape[0]
    rank = items_ref.shape[1]
    columns = long_lhs.shape[0]
    side_rows = columns // 2
    half_k = pair_ref.shape[2]
    depth = 2 * half_k

    def place(z_at, y_at, core_at):
        return (group, (z_at * 4 + y_at) * 2 + core_at)

    loads = [
        pltpu.make_async_copy(source, sink, load_sem.at[index])
        for index, (source, sink) in enumerate(
            ((aux_any, aux_ref), (items_any, items_ref), (basis_any, basis_ref), (pair_any, pair_ref))
        )
    ]
    for load in loads:
        load.start()

    sibling = place(z, y, 1 - core)
    z_peers = (place(wrap(z + 1), y, core), place(wrap(z - 1), y, core))
    turn = 2 * lax.rem(y, 2) - 1
    y_peers = (place(z, wrap(y + turn), core), place(z, wrap(y - turn), core))
    y_ahead = place(z, wrap(y + way), core)
    x_down = (z_low * 4 + wrap(x - way), member)
    x_up = (z_low * 4 + wrap(x + way), member)
    x_far = (z_low * 4 + wrap(x + 2), member)
    z_pair = ((1 - z_low) * 4 + x, member)
    seen_as = (2, 1)

    peers = z_peers + y_peers + (sibling, x_down, x_up, z_pair)
    barrier = pltpu.get_barrier_semaphore()
    for peer in peers:
        pl.semaphore_signal(barrier, inc=1, device_id=peer, device_id_type=MESH)
    loads[0].wait()
    for half in range(HALVES):
        own = aux_ref[half * piece : (half + 1) * piece]
        for part in range(2):
            factors[step_of(0, half), 0, core, :, part * half_k : (part + 1) * half_k] = own[:, part, :]
    pl.semaphore_wait(barrier, len(peers))

    waits = []

    def factor_copy(source, sink, target, send_sem):
        step, row = sink
        return pltpu.make_async_remote_copy(
            src_ref=factors.at[source[0], source[1], core],
            dst_ref=factors.at[step, row, core],
            send_sem=send_sem,
            recv_sem=factor_recv.at[(step * 4 + row) * 2 + core],
            device_id=target,
            device_id_type=MESH,
        )

    def send(source, sink, target, send_sem):
        copy = factor_copy(source, sink, target, send_sem)
        copy.start()
        waits.append(copy)

    def await_factor(step, row, core_at):
        pltpu.make_async_remote_copy(
            src_ref=factors.at[step, row, core_at],
            dst_ref=factors.at[step, row, core_at],
            send_sem=load_sem.at[0],
            recv_sem=factor_recv.at[(step * 4 + row) * 2 + core_at],
            device_id=sibling,
            device_id_type=MESH,
        ).wait_recv()

    def relay_copy(z_step, half):
        step = step_of(z_step, half)
        return factor_copy(
            (step, 0), (step_of(3, half), 0), z_peers[2 - z_step], z_relay.at[half]
        )

    def send_column(z_step, half):
        step = step_of(z_step, half)
        if z_step == 0:
            for index, target in enumerate(z_peers):
                sink = (step_of(seen_as[index], half), 0)
                send((step, 0), sink, target, z_send.at[half * 2 + index])
        else:
            await_factor(step, 0, core)
            if z_step < 3:

                @pl.when(core == 2 - z_step)
                def _():
                    relay_copy(z_step, half).start()

        for index, target in enumerate(y_peers):
            send((step, 0), (step, index + 1), target, y_send.at[step * 2 + index])
        send((step, 0), (step, 0), sibling, core_send.at[step * 4])

    def send_rows(z_step, half):
        step = step_of(z_step, half)
        behind = 1 + lax.rem(core + y, 2)
        await_factor(step, behind, core)
        send((step, behind), (step, 3), y_ahead, y_relay.at[step])
        send((step, behind), (step, behind), sibling, core_send.at[step * 4 + 1])
        await_factor(step, 3 - behind, core)
        send((step, 3 - behind), (step, 3 - behind), sibling, core_send.at[step * 4 + 2])

    def send_far(z_step, half):
        step = step_of(z_step, half)
        await_factor(step, 3, core)
        send((step, 3), (step, 3), sibling, core_send.at[step * 4 + 3])

    def prepare():
        loads[1].wait()

        slot = lax.broadcasted_iota(jnp.int32, (items, 128), 0)
        phases = jnp.zeros((items, 128), jnp.float32)
        reach = jnp.zeros((items, 128), jnp.float32)
        first = jnp.zeros((items, 128), jnp.float32)
        second = jnp.zeros((items, 128), jnp.float32)
        for index in range(items):
            alive = jnp.where(index < count_ref[0], 1.0, 0.0)
            to_second = sub_ref[index].astype(jnp.float32)
            phases = jnp.where(slot == index, phase_ref[image_ref[index]], phases)
            reach = jnp.where(slot == index, -dist_ref[image_ref[index]], reach)
            first = jnp.where(slot == index, alive * (1.0 - to_second), first)
            second = jnp.where(slot == index, alive * to_second, second)
        cosine, sine = jnp.cos(phases), jnp.sin(phases)
        scales[0] = cosine * first
        scales[1] = cosine * second
        scales[2] = sine * first
        scales[3] = sine * second

        def place_item(index, carry):
            block = items_ref[index].astype(jnp.float32).T
            at = pl.ds(pl.multiple_of(index * rank, rank), rank)
            for part in range(4):
                short_lhs[part * 128 : (part + 1) * 128, at] = (
                    block * scales[part, pl.ds(index, 1), :]
                ).astype(jnp.bfloat16)
            return carry

        lax.fori_loop(0, items, place_item, 0)

        loads[2].wait()

        def by_halves(left, right):
            low = lax.broadcasted_iota(jnp.int32, left.shape, 1) < piece
            return (
                jnp.where(low, left, pltpu.roll(right, piece, 1)),
                jnp.where(low, pltpu.roll(left, piece, 1), right),
            )

        def arrange(chip, carry):
            at = pl.multiple_of(chip * 256, 256)
            left, right = pl.ds(at, 128), pl.ds(at + 128, 128)
            basis_cols[:, left], basis_cols[:, right] = by_halves(
                basis_ref[:, left].astype(jnp.float32), basis_ref[:, right].astype(jnp.float32)
            )
            damping[:, left], damping[:, right] = by_halves(
                jnp.exp(reach * decay_ref[pl.ds(chip * 2, 1), :]),
                jnp.exp(reach * decay_ref[pl.ds(chip * 2 + 1, 1), :]),
            )
            return carry

        lax.fori_loop(0, basis_cols.shape[1] // 256, arrange, 0)

    def weigh():
        loads[3].wait()

        def rows_of(index, carry):
            at = pl.ds(pl.multiple_of(index * 32, 32), 32)
            low = pl.ds(pl.multiple_of(side_rows + index * 32, 32), 32)
            scaled = (pair_ref[at].astype(jnp.float32) * weight_ref[...][None]).astype(jnp.bfloat16)
            real_part, imag_part = scaled[:, 0, :], scaled[:, 1, :]
            long_lhs[at, 0:half_k] = real_part
            long_lhs[at, half_k:] = imag_part
            long_lhs[low, 0:half_k] = imag_part
            long_lhs[low, half_k:] = -real_part
            return carry

        lax.fori_loop(0, side_rows // 32, rows_of, 0)

    def short_range(z_step):
        def one(y_step, carry):
            chip = wrap(z + offset_of(z_step)) * 4 + wrap(y + turn * offset_of(y_step))
            at = pl.ds(pl.multiple_of(chip * 256, 256), 256)
            for index in range(items):
                damped[index * rank : (index + 1) * rank, :] = (
                    basis_cols[:, at] * damping[index : index + 1, at]
                ).astype(jnp.bfloat16)
            product = jnp.dot(short_lhs[...], damped[...], preferred_element_type=jnp.float32)
            for half in range(HALVES):
                total[step_of(z_step, half) * 4 + y_step] = product[:, half * 128 : (half + 1) * 128]
            return carry

        lax.fori_loop(0, SIDE, one, 0)

    def roles(z_step, row):
        z_at = wrap(z + offset_of(z_step))
        y_at = wrap(y + turn * offset_of(row))
        x_at = lax.rem(z_at, 2) * 2 + lax.div(y_at, 2)
        role = wrap((x - x_at) * way)
        return role, lax.div(z_at, 2) == z_low, lax.rem(y_at, 2)

    def reduce_copy(block, sink, recv_sem, target):
        return pltpu.make_async_remote_copy(
            src_ref=reduce_out.at[block],
            dst_ref=sink.at[block],
            send_sem=reduce_send.at[block],
            recv_sem=recv_sem.at[block],
            device_id=target,
            device_id_type=MESH,
        )

    def chain_copy(block):
        return reduce_copy(block, chain_in, chain_recv, x_down)

    def side_copy(block):
        return reduce_copy(block, side_in, side_recv, x_up)

    def far_copy(block):
        return reduce_copy(block, far_in, far_recv, x_far)

    def pair_copy(block):
        return reduce_copy(block, pair_in, pair_recv, z_pair)

    def long_range(quad):
        first_z, first_row, half = quad

        def one(pair, carry):
            z_step = first_z + pair
            step = step_of(z_step, half)
            for row in range(2):
                await_factor(step, first_row + row, 1 - core)
            rows = factors[step, first_row : first_row + 2].reshape(4 * piece, depth)
            product = lax.dot_general(
                long_lhs[...], rows, (((1,), (1,)), ((), ())), preferred_element_type=jnp.float32
            )
            for row in range(2):
                block = step * 4 + first_row + row
                total[block] += product[:, row * 128 : (row + 1) * 128]
                role, _, _ = roles(z_step, first_row + row)

                direct = quad in QUADS[len(QUADS) - DIRECT :]

                @pl.when(role >= (1 if direct else 2))
                def _():
                    reduce_out[block] = total[block].astype(jnp.bfloat16)

                @pl.when(role == (1 if direct else 2))
                def _():
                    chain_copy(block).start()

                if direct:

                    @pl.when(role == 2)
                    def _():
                        far_copy(block).start()

                @pl.when(role == 3)
                def _():
                    side_copy(block).start()

            return carry

        lax.fori_loop(0, 2, one, 0)

    def reduce_hop(quad, hop):
        first_z, first_row, half = quad
        direct = quad in QUADS[len(QUADS) - DIRECT :]
        if direct and hop == 1:
            return

        def one(index, carry):
            z_step = first_z + index // 2
            row = first_row + index % 2
            block = step_of(z_step, half) * 4 + row
            role, keeps, odd_y = roles(z_step, row)
            if hop == 1:

                @pl.when(role == 1)
                def _():
                    chain_copy(block).wait_recv()
                    reduce_out[block] = (total[block] + chain_in[block].astype(jnp.float32)).astype(
                        jnp.bfloat16
                    )
                    chain_copy(block).start()

            elif hop == 2:

                @pl.when(role == 0)
                def _():
                    side_copy(block).wait_recv()
                    chain_copy(block).wait_recv()
                    others = chain_in[block].astype(jnp.float32) + side_in[block].astype(jnp.float32)
                    if direct:
                        far_copy(block).wait_recv()
                        others += far_in[block].astype(jnp.float32)
                    total[block] += others

                @pl.when((role == 0) & jnp.logical_not(keeps))
                def _():
                    reduce_out[block] = total[block].astype(jnp.bfloat16)
                    pair_copy(block).start()

            else:

                @pl.when((role == 0) & keeps)
                def _():
                    pair_copy(block).wait_recv()
                    done = (total[block] + pair_in[block].astype(jnp.float32)).T
                    for core_at in range(2):
                        start = odd_y * (4 * piece) + (core_at * HALVES + half) * piece
                        out_ref[pl.ds(pl.multiple_of(start, piece), piece), :] = done[
                            core_at * piece : (core_at + 1) * piece
                        ].astype(jnp.bfloat16)

            return carry

        lax.fori_loop(0, SIDE, one, 0)

    def advance(index):
        def hop_of(hop):
            at = index - LAGS[hop - 1]
            if 0 <= at < len(QUADS):
                reduce_hop(QUADS[at], hop)

        hop_of(2)
        hop_of(3)
        if index < len(QUADS):
            long_range(QUADS[index])
        hop_of(1)

    send_column(0, 0)
    send_column(0, 1)
    prepare()
    short_range(0)
    send_rows(0, 0)
    send_rows(0, 1)
    send_column(1, 0)
    send_column(2, 0)
    weigh()
    short_range(1)
    send_far(0, 0)
    send_rows(1, 0)
    send_far(0, 1)
    send_column(1, 1)
    short_range(2)
    advance(0)
    send_rows(2, 0)
    send_far(1, 0)
    send_column(3, 0)
    send_column(2, 1)
    advance(1)
    short_range(3)
    send_rows(1, 1)
    send_column(3, 1)
    advance(2)
    send_far(2, 0)
    send_far(1, 1)
    send_rows(3, 0)
    advance(3)
    send_rows(2, 1)
    advance(4)
    send_far(3, 0)
    advance(5)
    send_rows(3, 1)
    send_far(2, 1)
    advance(6)
    send_far(3, 1)
    def drain(block, carry):
        role, keeps, _ = roles(block // (HALVES * SIDE), block % SIDE)

        @pl.when((role > 0) | jnp.logical_not(keeps))
        def _():
            chain_copy(block).wait_send()

        return carry

    advance(7)
    for copy in waits:
        copy.wait_send()
    for half in range(HALVES):
        relay_copy(1, half).wait_send()
    for index in range(8, len(QUADS) + LAGS[2]):
        advance(index)
        if index == 8:
            lax.fori_loop(0, STEPS * SIDE // 2, drain, 0)
    lax.fori_loop(STEPS * SIDE // 2, STEPS * SIDE, drain, 0)


def body(
    pair_ft,
    aux_ft,
    coul_weight,
    aux_basis,
    aux_decay,
    image_dist,
    image_phase,
    item_pair,
    item_image,
    item_sub,
    item_count,
):
    rows, _, depth = pair_ft.shape
    share = aux_ft.shape[0]
    aux_rows = aux_basis.shape[1]
    capacity, rank, _ = item_pair.shape
    columns = 2 * rows
    piece = share // HALVES
    blocks = STEPS * SIDE
    vmem = pl.BlockSpec(memory_space=pltpu.VMEM)
    smem = pl.BlockSpec(memory_space=pltpu.SMEM)
    dma = pltpu.SemaphoreType.DMA
    result = pl.pallas_call(
        kernel,
        out_shape=jax.ShapeDtypeStruct((aux_rows // lax.axis_size("grp"), columns), jnp.bfloat16),
        in_specs=[pl.BlockSpec(memory_space=pl.ANY)] * 4 + [vmem] * 2 + [smem] * 5,
        out_specs=vmem,
        scratch_shapes=[
            pltpu.VMEM((STEPS, SIDE, 2, piece, 2 * depth), jnp.bfloat16),
            pltpu.VMEM((blocks, columns, 2 * piece), jnp.float32),
            pltpu.VMEM((blocks, columns, 2 * piece), jnp.bfloat16),
            pltpu.VMEM((blocks, columns, 2 * piece), jnp.bfloat16),
            pltpu.VMEM((blocks, columns, 2 * piece), jnp.bfloat16),
            pltpu.VMEM((blocks, columns, 2 * piece), jnp.bfloat16),
            pltpu.VMEM((blocks, columns, 2 * piece), jnp.bfloat16),
            pltpu.VMEM((columns, 2 * depth), jnp.bfloat16),
            pltpu.VMEM((columns, capacity * rank), jnp.bfloat16),
            pltpu.VMEM((rank, aux_rows), jnp.float32),
            pltpu.VMEM((capacity, aux_rows), jnp.float32),
            pltpu.VMEM((capacity * rank, 2 * share), jnp.bfloat16),
            pltpu.VMEM((4, capacity, 128), jnp.float32),
            pltpu.VMEM((share, 2, depth), jnp.bfloat16),
            pltpu.VMEM((rows, 2, depth), jnp.bfloat16),
            pltpu.VMEM((rank, aux_rows), jnp.bfloat16),
            pltpu.VMEM((capacity, rank, 128), jnp.bfloat16),
            dma((4,)),
            dma((blocks * 2,)),
            dma((HALVES * 2,)),
            dma((HALVES,)),
            dma((STEPS * 2,)),
            dma((STEPS,)),
            dma((blocks,)),
            dma((blocks,)),
            dma((blocks,)),
            dma((blocks,)),
            dma((blocks,)),
            dma((blocks,)),
        ],
        compiler_params=pltpu.CompilerParams(
            collective_id=0, has_side_effects=True, vmem_limit_bytes=60 * 2**20
        ),
    )(
        aux_ft,
        pair_ft,
        aux_basis,
        item_pair,
        coul_weight.reshape(1, depth),
        aux_decay.reshape(aux_rows // 128, 128),
        image_dist,
        image_phase,
        item_image,
        item_sub,
        item_count,
    )
    return result.reshape(result.shape[0], 2, rows)


def solution(mesh):
    return jax.shard_map(
        body,
        mesh=mesh,
        in_specs=(
            P("dev", None, "grp"),
            P("dev", None, "grp"),
            P("grp"),
            P(),
            P(),
            P(),
            P(),
            P(("grp", "dev"), None, None),
            P(("grp", "dev")),
            P(("grp", "dev")),
            P(("grp", "dev")),
        ),
        out_specs=P("grp", None, "dev"),
        check_vma=False,
    )
```
